256 devices in a mesh: layer: 4 (over x_lo, core), space: 64 (over x_hi, y, z).
Axes of the slice: x: 4 (x_hi: 2, x_lo: 2; x = x_hi * 2 + x_lo), y: 4, z: 8, core: 2. Of those that a mesh axis runs over, the one named last changes fastest.
Arguments:
- states: bfloat16 [4, 512, 128, 256], P('layer', 'space'), may hold values from -6 to 6
- coarse_old: bfloat16 [4, 512, 128, 256], P('layer', 'space'), may hold values from -6 to 6
- fine_weights: bfloat16 [4, 3, 9, 256, 256], P('layer'), may hold values from -0.125 to 0.125
- coarse_weights: bfloat16 [4, 9, 256, 256], P('layer'), may hold values from -0.125 to 0.125
Outputs:
- end_states: bfloat16 [4, 512, 128, 256], P('layer', 'space')
- coarse_new: bfloat16 [4, 512, 128, 256], P('layer', 'space')
The draws below stay inside these ranges and needn't reach their ends.
All inputs are finite; a program needn't handle non-finite values.
Results may differ from the reference program's by a relative error of at most 0.008.
Values may be sent and summed in bfloat16 or wider, within the bound.
A program may use at most 64 MiB of HBM per device.

```python
import jax
import jax.numpy as jnp

CHANNELS = 256
COLS = 128
FINE = 3
GROUPS = 4
HEIGHT = 512


def block_scale(key, dims, pieces, smallest, largest):
    gain, own = 1.0, jax.random.fold_in(key, 6)
    for axis_at, parts in pieces:
        heights = jnp.exp(jax.random.uniform(jax.random.fold_in(own, axis_at), (parts,), jnp.float32, smallest / len(pieces), largest / len(pieces)))
        gain = gain * jnp.repeat(heights, dims[axis_at] // parts).reshape([-1 if axis == axis_at else 1 for axis in range(len(dims))])
    return gain


def gaussian(key, dims, spread, reach, split=(), kind=jnp.bfloat16):
    drawn = jax.random.normal(key, dims, jnp.float32) * spread
    if len(split) > 0:
        drawn = block_scale(key, dims, split, -0.22, 0.18) * drawn
    return jnp.clip(drawn, min=-reach, max=reach).astype(kind)


def setup_inputs(seed: int = 0) -> dict:
    key_list = jax.random.split(jax.random.key(seed), 5)
    states = gaussian(key_list[0], (GROUPS, HEIGHT, COLS, CHANNELS), 1.0, 6.0, ((0, 4), (1, 64)))
    coarse_old = gaussian(key_list[1], (GROUPS, HEIGHT, COLS, CHANNELS), 1.0, 6.0, ((0, 4), (1, 64)))
    fine_weights = gaussian(key_list[2], (GROUPS, FINE, 9, CHANNELS, CHANNELS), (9 * CHANNELS) ** -0.5, 0.125, ((0, 4),))
    coarse_weights = gaussian(key_list[3], (GROUPS, 9, CHANNELS, CHANNELS), (9 * CHANNELS) ** -0.5, 0.125, ((0, 4),))
    return {"states": states, "coarse_old": coarse_old, "fine_weights": fine_weights, "coarse_weights": coarse_weights}


def convolve(image, kernel):
    height_all, width_all, chans = image.shape
    padded = jnp.pad(image.astype(jnp.float32), ((1, 1), (1, 1), (0, 0)))
    summed = jnp.zeros((height_all * width_all, chans), jnp.float32)
    for position in range(9):
        row_step, col_step = divmod(position, 3)
        window = padded[row_step:row_step + height_all, col_step:col_step + width_all].reshape(-1, chans)
        summed = summed + jnp.dot(window, kernel[position].astype(jnp.float32))
    return summed.reshape(height_all, width_all, chans)


def reference(states, coarse_old, fine_weights, coarse_weights):
    group_count = states.shape[0]
    fine_list = []
    for group in range(group_count):
        field = states[group]
        for layer_no in range(FINE):
            field = (field.astype(jnp.float32) + jax.nn.relu(convolve(field, fine_weights[group, layer_no]))).astype(jnp.bfloat16)
        fine_list.append(field)
    entering = states[0]
    end_list = []
    coarse_list = []
    for group in range(group_count):
        coarse_val = entering.astype(jnp.float32) + jax.nn.relu(convolve(entering, coarse_weights[group]))
        coarse_list.append(coarse_val.astype(jnp.bfloat16))
        corrected = (coarse_val + (fine_list[group].astype(jnp.float32) - coarse_old[group].astype(jnp.float32))).astype(jnp.bfloat16)
        end_list.append(corrected)
        entering = corrected
    return jnp.stack(end_list), jnp.stack(coarse_list)
```

```python
import jax
import jax.numpy as jnp
from jax import lax
from jax.experimental import pallas as pl
from jax.experimental.pallas import tpu as pltpu
from jax.sharding import PartitionSpec as P

MESH = pl.DeviceIdType.MESH

RIM = 6
TOP, BOTTOM = RIM + 3, RIM + 4
LAG = (0, 2, 5, 4)


def pair_conv(read, weights, pair):
    taps = []
    for row_step in (-1, 0, 1):
        taps.append(
            jnp.concatenate(
                [read(TOP - pair + row_step), read(BOTTOM + pair + row_step)], axis=0
            )
        )
    window = jnp.concatenate(taps, axis=1)
    cols = taps[0].shape[0] // 2
    rows, chans = taps[0].shape
    parts = [
        jnp.dot(
            window,
            weights[step].reshape(3 * chans, chans),
            preferred_element_type=jnp.float32,
        )
        for step in range(3)
    ]
    col = lax.broadcasted_iota(jnp.int32, (rows, chans), 0) % cols
    left = jnp.where(col == 0, 0.0, pltpu.roll(parts[0], 1, 0))
    right = jnp.where(col == cols - 1, 0.0, pltpu.roll(parts[2], rows - 1, 0))
    total = parts[1] + left + right
    return taps[1].astype(jnp.float32) + jnp.maximum(total, 0.0)


def kernel(
    states, coarse_old, fine_w, coarse_w, end_out, coarse_out,
    field, level1, level2, fine, end, cold, weights,
    load_sem, weight_sem, halo_send, halo_recv, cold_send, cold_recv,
    end_send, end_recv,
):
    layer, space = lax.axis_index("layer"), lax.axis_index("space")
    groups, strips = lax.axis_size("layer"), lax.axis_size("space")
    cols = states.shape[2]
    has_above, has_below = space > 0, space < strips - 1
    has_prev, has_next = layer > 0, layer < groups - 1
    last = groups - 1 - layer + 3

    barrier = pltpu.get_barrier_semaphore()
    peers = (
        (has_above, (layer, space - 1)),
        (has_below, (layer, space + 1)),
        (has_prev, (layer - 1, space)),
        (has_next, (layer + 1, space)),
    )
    for present, peer in peers:
        @pl.when(present)
        def _(peer=peer):
            pl.semaphore_signal(barrier, inc=1, device_id=peer, device_id_type=MESH)

    greeted = sum(present.astype(jnp.int32) for present, _ in peers)

    load_field = pltpu.make_async_copy(
        states.at[0], field.at[0, pl.ds(RIM, 8)], load_sem.at[0]
    )
    load_field.start()
    loads = []
    for which in range(4):
        source = coarse_w if which == 3 else fine_w.at[0, which]
        source = source.at[0] if which == 3 else source
        loads.append(
            [
                pltpu.make_async_copy(
                    source.at[:, step], weights.at[which, step], weight_sem.at[which, step]
                )
                for step in range(3)
            ]
        )
    for group in loads[:3]:
        for copy in group:
            copy.start()
    load_cold = pltpu.make_async_copy(
        coarse_old.at[0], cold.at[pl.ds(RIM, 8)], load_sem.at[1]
    )
    for copy in loads[3]:
        copy.start()
    load_cold.start()

    def halo(ring, side, array, target, send, recv):
        row = 8 - ring if side == 0 else ring - 1
        slot = RIM - ring if side == 0 else RIM + 7 + ring
        return pltpu.make_async_remote_copy(
            src_ref=array.at[0, row],
            dst_ref=target.at[slot],
            send_sem=send.at[side, ring - 1],
            recv_sem=recv.at[side, ring - 1],
            device_id=(layer, space + 1 if side == 0 else space - 1),
            device_id_type=MESH,
        )

    def field_halo(ring, side):
        return halo(ring, side, states, field.at[0], halo_send, halo_recv)

    def cold_halo(ring, side):
        return halo(ring, side, coarse_old, cold, cold_send, cold_recv)

    def end_copy(pair, side):
        slot = TOP - pair if side == 0 else BOTTOM + pair
        return pltpu.make_async_remote_copy(
            src_ref=end.at[slot],
            dst_ref=field.at[1, slot],
            send_sem=end_send.at[side, pair],
            recv_sem=end_recv.at[side, pair],
            device_id=(layer + 1, space),
            device_id_type=MESH,
        )

    to, come = (has_below, has_above), (has_above, has_below)

    def keep(pair, value):
        top, bottom = value[:cols], value[cols:]
        top_in = has_above | (pair <= 3)
        bottom_in = has_below | (pair <= 3)
        return (
            jnp.where(top_in, top, 0.0).astype(jnp.bfloat16),
            jnp.where(bottom_in, bottom, 0.0).astype(jnp.bfloat16),
        )

    def fine_step(source, target, which, pair):
        value = pair_conv(lambda row: source[row], weights[which], pair)
        target[TOP - pair], target[BOTTOM + pair] = keep(pair, value)

    @pl.when(jnp.logical_not(has_above))
    def _():
        field[0, 0:RIM] = jnp.zeros((RIM, *field.shape[2:]), field.dtype)

    @pl.when(jnp.logical_not(has_below))
    def _():
        field[0, RIM + 8 :] = jnp.zeros((RIM, *field.shape[2:]), field.dtype)

    level0 = field.at[0]
    late = has_above & (space % 8 == 0)

    def prelude(part, carry):
        @pl.when((part == 0) != late)
        def _():
            pl.semaphore_wait(barrier, greeted)

            for side in (0, 1):
                @pl.when(to[side])
                def _(side=side):
                    @pl.loop(1, last + 1)
                    def _(ring):
                        field_halo(ring, side).start()

                    @pl.loop(1, last - 2)
                    def _(ring):
                        cold_halo(ring, side).start()

        @pl.when((part == 0) == late)
        def _():
            load_field.wait()
            for copy in loads[0]:
                copy.wait()
            fine_step(level0, level1, 0, 0)
            fine_step(level0, level1, 0, 1)
            for copy in loads[1]:
                copy.wait()
            fine_step(level1, level2, 1, 0)
            for copy in loads[2] + loads[3]:
                copy.wait()
            load_cold.wait()

        return carry

    lax.fori_loop(0, 2, prelude, 0)

    source_at = jnp.where(has_prev, 1, 0)
    lag = jnp.where(layer == 0, LAG[0], jnp.where(layer == 1, LAG[1], jnp.where(layer == 2, LAG[2], LAG[3])))

    def coarse_pair(pair):
        @pl.when(pair >= 4)
        def _():
            for side in (0, 1):
                @pl.when(come[side])
                def _(side=side):
                    cold_halo(pair - 3, side).wait_recv()

        @pl.when(has_prev)
        def _():
            @pl.when(pair == 0)
            def _():
                for side in (0, 1):
                    end_copy(0, side).wait_recv()

            for side in (0, 1):
                end_copy(pair + 1, side).wait_recv()

        entering = field.at[source_at]
        value = pair_conv(lambda row: entering[row], weights[3], pair)

        def both(ref):
            rows = jnp.concatenate([ref[TOP - pair], ref[BOTTOM + pair]], axis=0)
            return rows.astype(jnp.float32)

        leaving = keep(pair, value + (both(fine) - both(cold)))
        end[TOP - pair], end[BOTTOM + pair] = leaving

        @pl.when(has_next)
        def _():
            for side in (0, 1):
                end_copy(pair, side).start()

        @pl.when(pair <= 3)
        def _():
            end_out[0, 3 - pair], end_out[0, 4 + pair] = leaving
            coarse_out[0, 3 - pair] = value[:cols].astype(jnp.bfloat16)
            coarse_out[0, 4 + pair] = value[cols:].astype(jnp.bfloat16)

    @pl.loop(0, last + 1 + lag)
    def _(turn):
        @pl.when(turn <= last)
        def _():
            @pl.when(turn >= 1)
            def _():
                for side in (0, 1):
                    @pl.when(come[side])
                    def _(side=side):
                        field_halo(turn, side).wait_recv()

            fine_step(level0, level1, 0, turn + 2)
            fine_step(level1, level2, 1, turn + 1)
            fine_step(level2, fine, 2, turn)

        @pl.when(turn >= lag)
        def _():
            coarse_pair(turn - lag)

    for side in (0, 1):
        @pl.when(to[side])
        def _(side=side):
            @pl.loop(1, last + 1)
            def _(ring):
                field_halo(ring, side).wait_send()

            @pl.loop(1, last - 2)
            def _(ring):
                cold_halo(ring, side).wait_send()

        @pl.when(has_next)
        def _(side=side):
            @pl.loop(0, last + 1)
            def _(pair):
                end_copy(pair, side).wait_send()


def per_device(states, coarse_old, fine_weights, coarse_weights):
    _, rows, cols, chans = states.shape
    out = jax.ShapeDtypeStruct(states.shape, states.dtype)
    image = (rows + 2 * RIM, cols, chans)
    bf16 = jnp.bfloat16
    dma = pltpu.SemaphoreType.DMA
    return pl.pallas_call(
        kernel,
        out_shape=(out, out),
        in_specs=[pl.BlockSpec(memory_space=pl.ANY)] * 4,
        out_specs=[pl.BlockSpec(memory_space=pltpu.VMEM)] * 2,
        scratch_shapes=[
            pltpu.VMEM((2, *image), bf16),
            pltpu.VMEM(image, bf16),
            pltpu.VMEM(image, bf16),
            pltpu.VMEM(image, bf16),
            pltpu.VMEM(image, bf16),
            pltpu.VMEM(image, bf16),
            pltpu.VMEM((4, 3, 3, chans, chans), bf16),
            dma((2,)),
            dma((4, 3)),
            dma((2, 6)),
            dma((2, 6)),
            dma((2, 3)),
            dma((2, 3)),
            dma((2, 7)),
            dma((2, 7)),
        ],
        compiler_params=pltpu.CompilerParams(
            vmem_limit_bytes=56 << 20, collective_id=0, has_side_effects=True
        ),
    )(
        states,
        coarse_old,
        fine_weights.reshape(1, 3, 3, 3, chans, chans),
        coarse_weights.reshape(1, 3, 3, chans, chans),
    )


def solution(mesh):
    in_specs = (
        P("layer", "space", None, None),
        P("layer", "space", None, None),
        P("layer", None, None, None, None),
        P("layer", None, None, None),
    )
    out_specs = (P("layer", "space", None, None), P("layer", "space", None, None))
    return jax.shard_map(
        per_device, mesh=mesh, in_specs=in_specs, out_specs=out_specs, check_vma=False
    )
```

```python
import jax
import jax.numpy as jnp
from jax import lax
from jax.experimental import pallas as pl
from jax.experimental.pallas import tpu as pltpu
from jax.sharding import PartitionSpec as P

MESH = pl.DeviceIdType.MESH

RIM = 6
TOP, BOTTOM = RIM + 3, RIM + 4
LAG = 2


def conv_relu(source, weights, start, count):
    _, cols, chans = source.shape
    rows = count * cols
    taps = [
        source[pl.ds(start + row_step, count)].reshape(rows, chans)
        for row_step in (-1, 0, 1)
    ]
    window = jnp.concatenate(taps, axis=1)
    parts = [
        jnp.dot(
            window,
            weights[step].reshape(3 * chans, chans),
            preferred_element_type=jnp.float32,
        )
        for step in range(3)
    ]
    col = lax.broadcasted_iota(jnp.int32, (rows, chans), 0) % cols
    left = jnp.where(col == 0, 0.0, pltpu.roll(parts[0], 1, 0))
    right = jnp.where(col == cols - 1, 0.0, pltpu.roll(parts[2], rows - 1, 0))
    total = parts[1] + left + right
    return taps[1].astype(jnp.float32) + jnp.maximum(total, 0.0)


def kernel(
    states, coarse_old, fine_w, coarse_w, end_out, coarse_out,
    field, level1, level2, fine, end, cold, weights,
    load_sem, weight_sem, halo_send, halo_recv, cold_send, cold_recv,
    end_send, end_recv,
):
    layer, space = lax.axis_index("layer"), lax.axis_index("space")
    groups, strips = lax.axis_size("layer"), lax.axis_size("space")
    cols = states.shape[2]
    has_above, has_below = space > 0, space < strips - 1
    has_prev, has_next = layer > 0, layer < groups - 1
    last = groups - 1 - layer + 3

    barrier = pltpu.get_barrier_semaphore()
    peers = (
        (has_above, (layer, space - 1)),
        (has_below, (layer, space + 1)),
        (has_prev, (layer - 1, space)),
        (has_next, (layer + 1, space)),
    )
    for present, peer in peers:
        @pl.when(present)
        def _(peer=peer):
            pl.semaphore_signal(barrier, inc=1, device_id=peer, device_id_type=MESH)

    greeted = sum(present.astype(jnp.int32) for present, _ in peers)

    load_field = pltpu.make_async_copy(
        states.at[0], field.at[0, pl.ds(RIM, 8)], load_sem.at[0]
    )
    load_field.start()
    loads = []
    for which in range(4):
        source = coarse_w if which == 3 else fine_w.at[0, which]
        source = source.at[0] if which == 3 else source
        loads.append(
            [
                pltpu.make_async_copy(
                    source.at[:, step], weights.at[which, step], weight_sem.at[which, step]
                )
                for step in range(3)
            ]
        )
    for group in loads[:3]:
        for copy in group:
            copy.start()
    load_cold = pltpu.make_async_copy(
        coarse_old.at[0], cold.at[pl.ds(RIM, 8)], load_sem.at[1]
    )
    for copy in loads[3]:
        copy.start()
    load_cold.start()

    def pick(side, upper, lower):
        return jnp.where(side == 0, upper, lower)

    def slot_of(pair, side):
        return pick(side, TOP - pair, BOTTOM + pair)

    def halo(ring, side, array, target, send, recv):
        return pltpu.make_async_remote_copy(
            src_ref=array.at[0, pick(side, 8 - ring, ring - 1)],
            dst_ref=target.at[slot_of(3 + ring, side)],
            send_sem=send.at[side, ring - 1],
            recv_sem=recv.at[side, ring - 1],
            device_id=(layer, pick(side, space + 1, space - 1)),
            device_id_type=MESH,
        )

    def field_halo(ring, side):
        return halo(ring, side, states, field.at[0], halo_send, halo_recv)

    def cold_halo(ring, side):
        return halo(ring, side, coarse_old, cold, cold_send, cold_recv)

    def end_copy(pair, side):
        slot = slot_of(pair, side)
        return pltpu.make_async_remote_copy(
            src_ref=end.at[slot],
            dst_ref=field.at[1, slot],
            send_sem=end_send.at[side, pair],
            recv_sem=end_recv.at[side, pair],
            device_id=(layer + 1, space),
            device_id_type=MESH,
        )

    to = (has_below, has_above)

    def store(target, start, count, value):
        target[pl.ds(start, count)] = value.reshape(count, cols, -1).astype(target.dtype)

    def fine_rows(source, target, which, start, count):
        store(target, start, count, conv_relu(source, weights[which], start, count))

    def in_image(pair, side):
        return pick(side, has_above, has_below) | (pair <= 3)

    @pl.when(jnp.logical_not(has_above))
    def _():
        field[0, 0:RIM] = jnp.zeros((RIM, *field.shape[2:]), field.dtype)

    @pl.when(jnp.logical_not(has_below))
    def _():
        field[0, RIM + 8 :] = jnp.zeros((RIM, *field.shape[2:]), field.dtype)

    level0 = field.at[0]
    late_above = has_above & (space % 8 <= 1) & (space > 1)
    late_below = has_below & (space % 8 == 7)
    late = has_above & (space % 8 == 0)

    def prelude(part, carry):
        @pl.when((part == 0) != late)
        def _():
            pl.semaphore_wait(barrier, greeted)

            for side in (0, 1):
                @pl.when(to[side])
                def _(side=side):
                    @pl.loop(1, last + 1)
                    def _(ring):
                        field_halo(ring, side).start()

                    @pl.loop(1, last - 2)
                    def _(ring):
                        cold_halo(ring, side).start()

        @pl.when((part == 0) == late)
        def _():
            load_field.wait()
            for copy in loads[0]:
                copy.wait()
            for row in (1, 3, 5):
                fine_rows(level0, level1, 0, RIM + row, 2)
            for copy in loads[1]:
                copy.wait()
            for row in (2, 4):
                fine_rows(level1, level2, 1, RIM + row, 2)
            for copy in loads[2]:
                copy.wait()
            fine_rows(level2, fine, 2, RIM + 3, 2)
            for copy in loads[3]:
                copy.wait()
            load_cold.wait()

        return carry

    lax.fori_loop(0, 2, prelude, 0)

    apart = late_above | late_below
    late_side = late_below.astype(jnp.int32)
    halves = jnp.where(apart, 2, 1)

    def row_of(q):
        return jnp.where(q >= 0, q, -1 - q), jnp.where(q >= 0, late_side, 1 - late_side)

    def fine_at(half, step):
        _, side = row_of(jnp.where(half == 0, -1, 0))
        pair = jnp.where(apart, step, step // 2) + 1
        return pair, jnp.where(apart, side, step % 2)

    def coarse_q(half, step):
        return jnp.where(half == 0, -layer - step, step - layer + 1)

    def coarse_at(half, step):
        pair, side = row_of(coarse_q(half, step))
        return jnp.where(apart, pair, step // 2), jnp.where(apart, side, step % 2)

    def fine_step(source, target, which, pair, side):
        slot = slot_of(pair, side)
        value = conv_relu(source, weights[which], slot, 1)
        store(target, slot, 1, jnp.where(in_image(pair, side), value, 0.0))

    def await_ring(half, step):
        ring, side = fine_at(half, step)

        @pl.when(pick(side, has_above, has_below))
        def _():
            field_halo(ring, side).wait_recv()

    def fine_turn(half, step):
        pair, side = fine_at(half, step)
        fine_step(level0, level1, 0, pair + 2, side)
        fine_step(level1, level2, 1, pair + 1, side)
        fine_step(level2, fine, 2, pair, side)

    source_at = jnp.where(has_prev, 1, 0)
    def await_end(pair, side):
        end_copy(pair, side).wait_recv()

    def await_entering(half, step):
        pair, side = coarse_at(half, step)

        @pl.when((pair >= 4) & pick(side, has_above, has_below))
        def _():
            cold_halo(pair - 3, side).wait_recv()

        first = (half == 0) & (step == 0)

        @pl.when(has_prev & apart)
        def _():
            q = coarse_q(half, step)

            @pl.when(first)
            def _():
                await_end(*row_of(q + 1))
                await_end(*row_of(q))

            await_end(*row_of(jnp.where(half == 0, q - 1, q + 1)))

        @pl.when(has_prev & jnp.logical_not(apart))
        def _():
            @pl.when(first)
            def _():
                for early in (0, 1):
                    await_end(0, early)
                    await_end(1, early)

            @pl.when(step >= 2)
            def _():
                await_end(pair + 1, side)

    def coarse_turn(half, step):
        pair, side = coarse_at(half, step)
        slot = slot_of(pair, side)
        value = conv_relu(field.at[source_at], weights[3], slot, 1)

        def row(ref):
            return ref[slot].astype(jnp.float32)

        leaving = value + (row(fine) - row(cold))
        leaving = jnp.where(in_image(pair, side), leaving, 0.0)
        store(end, slot, 1, leaving)

        @pl.when(has_next)
        def _():
            end_copy(pair, side).start()

        @pl.when(pair <= 3)
        def _():
            store(end_out.at[0], slot - RIM, 1, leaving)
            store(coarse_out.at[0], slot - RIM, 1, value)

    @pl.loop(0, halves)
    def _(half):
        n_fine = jnp.where(apart, last, 2 * last)
        n_coarse = jnp.where(half == 0, 8 - 2 * layer, last + layer)
        n_coarse = jnp.where(apart, n_coarse, 2 * last + 2)
        lag = jnp.where(layer == 0, jnp.where(half == 0, -2, 0), LAG)
        lag = jnp.where(layer >= 2, n_fine, lag)

        @pl.loop(0, jnp.maximum(-lag, 0))
        def _(step):
            coarse_turn(half, step)

        @pl.loop(0, jnp.maximum(lag, 0))
        def _(step):
            await_ring(half, step)
            fine_turn(half, step)

        @pl.loop(jnp.maximum(lag, 0), n_fine)
        def _(step):
            await_ring(half, step)
            await_entering(half, step - lag)
            fine_turn(half, step)
            coarse_turn(half, step - lag)

        @pl.loop(n_fine - lag, n_coarse)
        def _(step):
            await_entering(half, step)
            coarse_turn(half, step)

    for side in (0, 1):
        @pl.when(to[side])
        def _(side=side):
            @pl.loop(1, last + 1)
            def _(ring):
                field_halo(ring, side).wait_send()

            @pl.loop(1, last - 2)
            def _(ring):
                cold_halo(ring, side).wait_send()

        @pl.when(has_next)
        def _(side=side):
            @pl.loop(0, last + 1)
            def _(pair):
                end_copy(pair, side).wait_send()


def hand_over(end, coarse, end_out, coarse_out, sem):
    copies = [
        pltpu.make_async_copy(end, end_out, sem.at[0]),
        pltpu.make_async_copy(coarse, coarse_out, sem.at[1]),
    ]
    for copy in copies:
        copy.start()
    for copy in copies:
        copy.wait()


def per_device(states, coarse_old, fine_weights, coarse_weights):
    _, rows, cols, chans = states.shape
    out = jax.ShapeDtypeStruct(states.shape, states.dtype)
    image = (rows + 2 * RIM, cols, chans)
    bf16 = jnp.bfloat16
    dma = pltpu.SemaphoreType.DMA
    def stay(array):
        return pltpu.with_memory_space_constraint(array, pltpu.HBM)

    results = pl.pallas_call(
        kernel,
        out_shape=(out, out),
        in_specs=[pl.BlockSpec(memory_space=pl.ANY)] * 4,
        out_specs=[pl.BlockSpec(memory_space=pltpu.VMEM)] * 2,
        scratch_shapes=[
            pltpu.VMEM((2, *image), bf16),
            pltpu.VMEM(image, bf16),
            pltpu.VMEM(image, bf16),
            pltpu.VMEM(image, bf16),
            pltpu.VMEM(image, bf16),
            pltpu.VMEM(image, bf16),
            pltpu.VMEM((4, 3, 3, chans, chans), bf16),
            dma((2,)),
            dma((4, 3)),
            dma((2, 6)),
            dma((2, 6)),
            dma((2, 3)),
            dma((2, 3)),
            dma((2, 7)),
            dma((2, 7)),
        ],
        compiler_params=pltpu.CompilerParams(
            vmem_limit_bytes=40 << 20, collective_id=0, has_side_effects=True
        ),
    )(
        stay(states),
        stay(coarse_old),
        stay(fine_weights.reshape(1, 3, 3, 3, chans, chans)),
        stay(coarse_weights.reshape(1, 3, 3, chans, chans)),
    )
    return pl.pallas_call(
        hand_over,
        out_shape=(out, out),
        in_specs=[pl.BlockSpec(memory_space=pl.ANY)] * 2,
        out_specs=[pl.BlockSpec(memory_space=pl.ANY)] * 2,
        scratch_shapes=[dma((2,))],
        compiler_params=pltpu.CompilerParams(vmem_limit_bytes=1 << 20),
    )(*results)


def solution(mesh):
    in_specs = (
        P("layer", "space", None, None),
        P("layer", "space", None, None),
        P("layer", None, None, None, None),
        P("layer", None, None, None),
    )
    out_specs = (P("layer", "space", None, None), P("layer", "space", None, None))
    return jax.shard_map(
        per_device, mesh=mesh, in_specs=in_specs, out_specs=out_specs, check_vma=False
    )
```

```python
import jax
import jax.numpy as jnp
from jax import lax
from jax.experimental import pallas as pl
from jax.experimental.pallas import tpu as pltpu
from jax.sharding import PartitionSpec as P

MESH = pl.DeviceIdType.MESH

RIM = 6
TOP, BOTTOM = RIM + 3, RIM + 4
LAG = 4


def conv_relu(source, weights, start, count):
    _, cols, chans = source.shape
    rows = count * cols
    taps = [
        source[pl.ds(start + row_step, count)].reshape(rows, chans)
        for row_step in (-1, 0, 1)
    ]
    window = jnp.concatenate(taps, axis=1)
    parts = [
        jnp.dot(
            window,
            weights[step].reshape(3 * chans, chans),
            preferred_element_type=jnp.float32,
        )
        for step in range(3)
    ]
    col = lax.broadcasted_iota(jnp.int32, (rows, chans), 0) % cols
    left = jnp.where(col == 0, 0.0, pltpu.roll(parts[0], 1, 0))
    right = jnp.where(col == cols - 1, 0.0, pltpu.roll(parts[2], rows - 1, 0))
    total = parts[1] + left + right
    return taps[1].astype(jnp.float32) + jnp.maximum(total, 0.0)


def kernel(
    states, coarse_old, fine_w, coarse_w, end, coarse,
    field, level1, level2, fine, cold, weights,
    load_sem, weight_sem, halo_send, halo_recv, cold_send, cold_recv,
    end_send, end_recv,
):
    layer, space = lax.axis_index("layer"), lax.axis_index("space")
    groups, strips = lax.axis_size("layer"), lax.axis_size("space")
    cols = states.shape[2]
    has_above, has_below = space > 0, space < strips - 1
    has_prev, has_next = layer > 0, layer < groups - 1
    last = groups - 1 - layer + 3

    barrier = pltpu.get_barrier_semaphore()
    peers = (
        (has_above, (layer, space - 1)),
        (has_below, (layer, space + 1)),
        (has_prev, (layer - 1, space)),
        (has_next, (layer + 1, space)),
    )
    for present, peer in peers:
        @pl.when(present)
        def _(peer=peer):
            pl.semaphore_signal(barrier, inc=1, device_id=peer, device_id_type=MESH)

    greeted = sum(present.astype(jnp.int32) for present, _ in peers)

    load_field = pltpu.make_async_copy(
        states.at[0], field.at[0, pl.ds(RIM, 8)], load_sem.at[0]
    )
    load_field.start()
    loads = []
    for which in range(4):
        source = coarse_w if which == 3 else fine_w.at[0, which]
        source = source.at[0] if which == 3 else source
        loads.append(
            [
                pltpu.make_async_copy(
                    source.at[:, step], weights.at[which, step], weight_sem.at[which, step]
                )
                for step in range(3)
            ]
        )
    for group in loads[:3]:
        for copy in group:
            copy.start()
    load_cold = pltpu.make_async_copy(
        coarse_old.at[0], cold.at[pl.ds(RIM, 8)], load_sem.at[1]
    )
    for copy in loads[3]:
        copy.start()
    load_cold.start()

    def pick(side, upper, lower):
        return jnp.where(side == 0, upper, lower)

    def slot_of(pair, side):
        return pick(side, TOP - pair, BOTTOM + pair)

    def halo(ring, side, array, target, send, recv):
        return pltpu.make_async_remote_copy(
            src_ref=array.at[0, pick(side, 8 - ring, ring - 1)],
            dst_ref=target.at[slot_of(3 + ring, side)],
            send_sem=send.at[side, ring - 1],
            recv_sem=recv.at[side, ring - 1],
            device_id=(layer, pick(side, space + 1, space - 1)),
            device_id_type=MESH,
        )

    def field_halo(ring, side):
        return halo(ring, side, states, field.at[0], halo_send, halo_recv)

    def cold_halo(ring, side):
        return halo(ring, side, coarse_old, cold, cold_send, cold_recv)

    def end_copy(pair, side):
        slot = slot_of(pair, side)
        return pltpu.make_async_remote_copy(
            src_ref=end.at[slot],
            dst_ref=field.at[1, slot],
            send_sem=end_send.at[side, pair],
            recv_sem=end_recv.at[side, pair],
            device_id=(layer + 1, space),
            device_id_type=MESH,
        )

    to = (has_below, has_above)

    def store(target, start, count, value):
        target[pl.ds(start, count)] = value.reshape(count, cols, -1).astype(target.dtype)

    def fine_rows(source, target, which, start, count):
        store(target, start, count, conv_relu(source, weights[which], start, count))

    def in_image(pair, side):
        return pick(side, has_above, has_below) | (pair <= 3)

    @pl.when(jnp.logical_not(has_above))
    def _():
        field[0, 0:RIM] = jnp.zeros((RIM, *field.shape[2:]), field.dtype)

    @pl.when(jnp.logical_not(has_below))
    def _():
        field[0, RIM + 8 :] = jnp.zeros((RIM, *field.shape[2:]), field.dtype)

    level0 = field.at[0]
    late_above = has_above & (space % 8 <= 1) & (space > 1)
    late_below = has_below & (space % 8 == 7)
    late = has_above & (space % 8 == 0)

    def prelude(part, carry):
        @pl.when((part == 0) != late)
        def _():
            pl.semaphore_wait(barrier, greeted)

            for side in (0, 1):
                @pl.when(to[side])
                def _(side=side):
                    @pl.loop(1, last + 1)
                    def _(ring):
                        field_halo(ring, side).start()

                    @pl.loop(1, last - 2)
                    def _(ring):
                        cold_halo(ring, side).start()

        @pl.when((part == 0) == late)
        def _():
            load_field.wait()
            for copy in loads[0]:
                copy.wait()
            for row in (1, 3, 5):
                fine_rows(level0, level1, 0, RIM + row, 2)
            for copy in loads[1]:
                copy.wait()
            for row in (2, 4):
                fine_rows(level1, level2, 1, RIM + row, 2)
            for copy in loads[2]:
                copy.wait()
            fine_rows(level2, fine, 2, RIM + 3, 2)
            for copy in loads[3]:
                copy.wait()
            load_cold.wait()

        return carry

    lax.fori_loop(0, 2, prelude, 0)

    apart = late_above | late_below
    late_side = late_below.astype(jnp.int32)
    halves = jnp.where(apart, 2, 1)

    def row_of(q):
        return jnp.where(q >= 0, q, -1 - q), jnp.where(q >= 0, late_side, 1 - late_side)

    def fine_at(half, step):
        _, side = row_of(jnp.where(half == 0, -1, 0))
        pair = jnp.where(apart, step, step // 2) + 1
        return pair, jnp.where(apart, side, step % 2)

    def coarse_q(half, step):
        return jnp.where(half == 0, -layer - step, step - layer + 1)

    def coarse_at(half, step):
        pair, side = row_of(coarse_q(half, step))
        return jnp.where(apart, pair, step // 2), jnp.where(apart, side, step % 2)

    def fine_step(source, target, which, pair, side):
        slot = slot_of(pair, side)
        value = conv_relu(source, weights[which], slot, 1)
        store(target, slot, 1, jnp.where(in_image(pair, side), value, 0.0))

    def await_ring(half, step):
        ring, side = fine_at(half, step)

        @pl.when(pick(side, has_above, has_below))
        def _():
            field_halo(ring, side).wait_recv()

    def first_layer(half, step):
        pair, side = fine_at(half, step)
        fine_step(level0, level1, 0, pair + 2, side)

    def second_layer(half, step):
        pair, side = fine_at(half, step - 1)
        fine_step(level1, level2, 1, pair + 1, side)

    def third_layer(half, step):
        pair, side = fine_at(half, step - 2)
        fine_step(level2, fine, 2, pair, side)

    source_at = jnp.where(has_prev, 1, 0)
    def await_end(pair, side):
        end_copy(pair, side).wait_recv()

    def await_entering(half, step):
        pair, side = coarse_at(half, step)

        @pl.when((pair >= 4) & pick(side, has_above, has_below))
        def _():
            cold_halo(pair - 3, side).wait_recv()

        first = (half == 0) & (step == 0)

        @pl.when(has_prev & apart)
        def _():
            q = coarse_q(half, step)

            @pl.when(first)
            def _():
                await_end(*row_of(q + 1))
                await_end(*row_of(q))

            await_end(*row_of(jnp.where(half == 0, q - 1, q + 1)))

        @pl.when(has_prev & jnp.logical_not(apart))
        def _():
            @pl.when(first)
            def _():
                for early in (0, 1):
                    await_end(0, early)
                    await_end(1, early)

            @pl.when(step >= 2)
            def _():
                await_end(pair + 1, side)

    def coarse_row(half, step):
        pair, side = coarse_at(half, step)
        slot = slot_of(pair, side)
        value = conv_relu(field.at[source_at], weights[3], slot, 1)

        def row(ref):
            return ref[slot].astype(jnp.float32)

        leaving = value + (row(fine) - row(cold))
        store(end, slot, 1, jnp.where(in_image(pair, side), leaving, 0.0))
        store(coarse, slot, 1, value)

    def send_on(half, step):
        @pl.when(has_next)
        def _():
            end_copy(*coarse_at(half, step)).start()

    @pl.loop(0, halves)
    def _(half):
        n_fine = jnp.where(apart, last, 2 * last)
        n_coarse = jnp.where(half == 0, 8 - 2 * layer, last + layer)
        n_coarse = jnp.where(apart, n_coarse, 2 * last + 2)
        lag = jnp.where(layer == 0, jnp.where(half == 0, 0, 2), LAG)
        lag = jnp.where(layer >= 2, n_fine + 2, lag)

        @pl.loop(0, jnp.minimum(lag, n_fine))
        def _(step):
            await_ring(half, step)
            third_layer(half, step)
            second_layer(half, step)
            first_layer(half, step)

        @pl.loop(lag, n_fine)
        def _(step):
            await_ring(half, step)
            await_entering(half, step - lag)
            third_layer(half, step)
            coarse_row(half, step - lag)
            second_layer(half, step)
            first_layer(half, step)
            send_on(half, step - lag)

        @pl.when(lag <= n_fine)
        def _():
            await_entering(half, n_fine - lag)
            third_layer(half, n_fine)
            coarse_row(half, n_fine - lag)
            second_layer(half, n_fine)
            send_on(half, n_fine - lag)
            await_entering(half, n_fine + 1 - lag)
            third_layer(half, n_fine + 1)
            coarse_row(half, n_fine + 1 - lag)
            send_on(half, n_fine + 1 - lag)

        @pl.when(lag > n_fine)
        def _():
            third_layer(half, n_fine)
            second_layer(half, n_fine)
            third_layer(half, n_fine + 1)

        @pl.loop(n_fine + 2 - lag, n_coarse)
        def _(step):
            await_entering(half, step)
            coarse_row(half, step)
            send_on(half, step)

    for side in (0, 1):
        @pl.when(to[side])
        def _(side=side):
            @pl.loop(1, last + 1)
            def _(ring):
                field_halo(ring, side).wait_send()

            @pl.loop(1, last - 2)
            def _(ring):
                cold_halo(ring, side).wait_send()

        @pl.when(has_next)
        def _(side=side):
            @pl.loop(0, last + 1)
            def _(pair):
                end_copy(pair, side).wait_send()


def hand_over(end, coarse, end_out, coarse_out, sem):
    rows = pl.ds(RIM, end_out.shape[1])
    copies = [
        pltpu.make_async_copy(end.at[rows], end_out.at[0], sem.at[0]),
        pltpu.make_async_copy(coarse.at[rows], coarse_out.at[0], sem.at[1]),
    ]
    for copy in copies:
        copy.start()
    for copy in copies:
        copy.wait()


def per_device(states, coarse_old, fine_weights, coarse_weights):
    _, rows, cols, chans = states.shape
    out = jax.ShapeDtypeStruct(states.shape, states.dtype)
    image = (rows + 2 * RIM, cols, chans)
    bf16 = jnp.bfloat16
    dma = pltpu.SemaphoreType.DMA
    def stay(array):
        return pltpu.with_memory_space_constraint(array, pltpu.HBM)

    results = pl.pallas_call(
        kernel,
        out_shape=(jax.ShapeDtypeStruct(image, bf16),) * 2,
        in_specs=[pl.BlockSpec(memory_space=pl.ANY)] * 4,
        out_specs=[pl.BlockSpec(memory_space=pltpu.VMEM)] * 2,
        scratch_shapes=[
            pltpu.VMEM((2, *image), bf16),
            pltpu.VMEM(image, bf16),
            pltpu.VMEM(image, bf16),
            pltpu.VMEM(image, bf16),
            pltpu.VMEM(image, bf16),
            pltpu.VMEM((4, 3, 3, chans, chans), bf16),
            dma((2,)),
            dma((4, 3)),
            dma((2, 6)),
            dma((2, 6)),
            dma((2, 3)),
            dma((2, 3)),
            dma((2, 7)),
            dma((2, 7)),
        ],
        compiler_params=pltpu.CompilerParams(
            vmem_limit_bytes=40 << 20, collective_id=0, has_side_effects=True
        ),
    )(
        stay(states),
        stay(coarse_old),
        stay(fine_weights.reshape(1, 3, 3, 3, chans, chans)),
        stay(coarse_weights.reshape(1, 3, 3, chans, chans)),
    )
    return pl.pallas_call(
        hand_over,
        out_shape=(out, out),
        in_specs=[pl.BlockSpec(memory_space=pl.ANY)] * 2,
        out_specs=[pl.BlockSpec(memory_space=pl.ANY)] * 2,
        scratch_shapes=[dma((2,))],
        compiler_params=pltpu.CompilerParams(vmem_limit_bytes=1 << 20),
    )(*results)


def solution(mesh):
    in_specs = (
        P("layer", "space", None, None),
        P("layer", "space", None, None),
        P("layer", None, None, None, None),
        P("layer", None, None, None),
    )
    out_specs = (P("layer", "space", None, None), P("layer", "space", None, None))
    return jax.shard_map(
        per_device, mesh=mesh, in_specs=in_specs, out_specs=out_specs, check_vma=False
    )
```

```python
import jax
import jax.numpy as jnp
from jax import lax
from jax.experimental import pallas as pl
from jax.experimental.pallas import tpu as pltpu
from jax.sharding import PartitionSpec as P

MESH = pl.DeviceIdType.MESH

RIM = 6
TOP, BOTTOM = RIM + 3, RIM + 4
LAG = 4


def conv_relu(source, weights, start, count):
    _, cols, chans = source.shape
    rows = count * cols
    taps = [
        source[pl.ds(start + row_step, count)].reshape(rows, chans)
        for row_step in (-1, 0, 1)
    ]
    window = jnp.concatenate(taps, axis=1)
    parts = [
        jnp.dot(
            window,
            weights[step].reshape(3 * chans, chans),
            preferred_element_type=jnp.float32,
        )
        for step in range(3)
    ]
    col = lax.broadcasted_iota(jnp.int32, (rows, chans), 0) % cols
    left = jnp.where(col == 0, 0.0, pltpu.roll(parts[0], 1, 0))
    right = jnp.where(col == cols - 1, 0.0, pltpu.roll(parts[2], rows - 1, 0))
    total = parts[1] + left + right
    return taps[1].astype(jnp.float32) + jnp.maximum(total, 0.0)


def kernel(
    states, coarse_old, fine_w, coarse_w, end, coarse,
    field, level1, level2, fine, cold, weights,
    load_sem, weight_sem, halo_send, halo_recv, cold_send, cold_recv,
    end_send, end_recv, relay, relay_send, relay_recv, forward_send,
):
    layer, space = lax.axis_index("layer"), lax.axis_index("space")
    groups, strips = lax.axis_size("layer"), lax.axis_size("space")
    cols = states.shape[2]
    has_above, has_below = space > 0, space < strips - 1
    has_prev, has_next = layer > 0, layer < groups - 1
    last = groups - 1 - layer + 3

    first_two = layer < 2
    partner = jnp.where(first_two, layer + 2, layer - 2)
    relayed = jnp.where(first_two, 3 - layer, 5 - layer)
    leaves, enters = space == strips // 2 - 1, space == strips // 2

    barrier = pltpu.get_barrier_semaphore()
    peers = (
        (has_above, (layer, space - 1)),
        (has_below, (layer, space + 1)),
        (has_prev, (layer - 1, space)),
        (has_next, (layer + 1, space)),
        (leaves | enters, (partner, space)),
    )
    for present, peer in peers:
        @pl.when(present)
        def _(peer=peer):
            pl.semaphore_signal(barrier, inc=1, device_id=peer, device_id_type=MESH)

    greeted = sum(present.astype(jnp.int32) for present, _ in peers)

    load_field = pltpu.make_async_copy(
        states.at[0], field.at[0, pl.ds(RIM, 8)], load_sem.at[0]
    )
    load_field.start()
    loads = []
    for which in range(4):
        source = coarse_w if which == 3 else fine_w.at[0, which]
        source = source.at[0] if which == 3 else source
        loads.append(
            [
                pltpu.make_async_copy(
                    source.at[:, step], weights.at[which, step], weight_sem.at[which, step]
                )
                for step in range(3)
            ]
        )
    for group in loads[:3]:
        for copy in group:
            copy.start()
    load_cold = pltpu.make_async_copy(
        coarse_old.at[0], cold.at[pl.ds(RIM, 8)], load_sem.at[1]
    )
    for copy in loads[3]:
        copy.start()
    load_cold.start()

    def pick(side, upper, lower):
        return jnp.where(side == 0, upper, lower)

    def slot_of(pair, side):
        return pick(side, TOP - pair, BOTTOM + pair)

    def halo(ring, side, array, target, send, recv):
        return pltpu.make_async_remote_copy(
            src_ref=array.at[0, pick(side, 8 - ring, ring - 1)],
            dst_ref=target.at[slot_of(3 + ring, side)],
            send_sem=send.at[side, ring - 1],
            recv_sem=recv.at[side, ring - 1],
            device_id=(layer, pick(side, space + 1, space - 1)),
            device_id_type=MESH,
        )

    def field_halo(ring, side):
        return halo(ring, side, states, field.at[0], halo_send, halo_recv)

    def cold_halo(ring, side):
        return halo(ring, side, coarse_old, cold, cold_send, cold_recv)

    def detour(ring, source, target, send, recv, device):
        return pltpu.make_async_remote_copy(
            src_ref=source,
            dst_ref=target,
            send_sem=send.at[ring - 1],
            recv_sem=recv,
            device_id=device,
            device_id_type=MESH,
        )

    def to_relay(ring):
        return detour(
            ring, coarse_old.at[0, 8 - ring], relay.at[ring - 1],
            relay_send, relay_recv.at[ring - 1], (partner, space),
        )

    def over_cut(ring):
        return detour(
            ring, relay.at[ring - 1], relay.at[ring - 1],
            forward_send, relay_recv.at[ring - 1], (layer, space + 1),
        )

    def from_relay(ring):
        return detour(
            ring, relay.at[ring - 1], cold.at[TOP - 3 - ring],
            forward_send, cold_recv.at[0, ring - 1], (partner, space),
        )

    def rings(condition, start, stop, act):
        @pl.when(condition)
        def _():
            @pl.loop(start, stop)
            def _(ring):
                act(ring)

    relays = leaves & jnp.logical_not(first_two)
    returns = enters & jnp.logical_not(first_two)
    detours = leaves & first_two

    def end_copy(pair, side):
        slot = slot_of(pair, side)
        return pltpu.make_async_remote_copy(
            src_ref=end.at[slot],
            dst_ref=field.at[1, slot],
            send_sem=end_send.at[side, pair],
            recv_sem=end_recv.at[side, pair],
            device_id=(layer + 1, space),
            device_id_type=MESH,
        )

    to = (has_below, has_above)

    def store(target, start, count, value):
        target[pl.ds(start, count)] = value.reshape(count, cols, -1).astype(target.dtype)

    def fine_rows(source, target, which, start, count):
        store(target, start, count, conv_relu(source, weights[which], start, count))

    def in_image(pair, side):
        return pick(side, has_above, has_below) | (pair <= 3)

    @pl.when(jnp.logical_not(has_above))
    def _():
        field[0, 0:RIM] = jnp.zeros((RIM, *field.shape[2:]), field.dtype)

    @pl.when(jnp.logical_not(has_below))
    def _():
        field[0, RIM + 8 :] = jnp.zeros((RIM, *field.shape[2:]), field.dtype)

    level0 = field.at[0]
    late_above = has_above & (space % 8 <= 1) & (space > 1)
    late_below = has_below & (space % 8 == 7)
    late = has_above & (space % 8 == 0)

    def prelude(part, carry):
        @pl.when((part == 0) != late)
        def _():
            pl.semaphore_wait(barrier, greeted)

            def pass_on(ring):
                to_relay(ring).wait_recv()
                over_cut(ring).start()

            split = jnp.where(relays, 3, last + 1)
            rings(detours, 1, relayed + 1, lambda ring: to_relay(ring).start())
            rings(to[0], 1, split, lambda ring: field_halo(ring, 0).start())
            rings(to[1], 1, last + 1, lambda ring: field_halo(ring, 1).start())
            rings(to[1], 1, last - 2, lambda ring: cold_halo(ring, 1).start())
            rings(relays, 1, relayed + 1, pass_on)
            rings(to[0], split, last + 1, lambda ring: field_halo(ring, 0).start())
            rings(
                to[0] & jnp.logical_not(detours), 1, last - 2,
                lambda ring: cold_halo(ring, 0).start(),
            )

        @pl.when((part == 0) == late)
        def _():
            load_field.wait()
            for copy in loads[0]:
                copy.wait()
            for row in (1, 3, 5):
                fine_rows(level0, level1, 0, RIM + row, 2)
            for copy in loads[1]:
                copy.wait()
            for row in (2, 4):
                fine_rows(level1, level2, 1, RIM + row, 2)
            for copy in loads[2]:
                copy.wait()
            fine_rows(level2, fine, 2, RIM + 3, 2)
            for copy in loads[3]:
                copy.wait()
            load_cold.wait()

        return carry

    lax.fori_loop(0, 2, prelude, 0)

    apart = late_above | late_below
    late_side = late_below.astype(jnp.int32)
    halves = jnp.where(apart, 2, 1)

    def row_of(q):
        return jnp.where(q >= 0, q, -1 - q), jnp.where(q >= 0, late_side, 1 - late_side)

    def fine_at(half, step):
        _, side = row_of(jnp.where(half == 0, -1, 0))
        pair = jnp.where(apart, step, step // 2) + 1
        return pair, jnp.where(apart, side, step % 2)

    def coarse_q(half, step):
        return jnp.where(half == 0, -layer - step, step - layer + 1)

    def coarse_at(half, step):
        pair, side = row_of(coarse_q(half, step))
        return jnp.where(apart, pair, step // 2), jnp.where(apart, side, step % 2)

    def fine_step(source, target, which, pair, side):
        slot = slot_of(pair, side)
        value = conv_relu(source, weights[which], slot, 1)
        store(target, slot, 1, jnp.where(in_image(pair, side), value, 0.0))

    def await_ring(half, step):
        ring, side = fine_at(half, step)

        @pl.when(pick(side, has_above, has_below))
        def _():
            field_halo(ring, side).wait_recv()

    def first_layer(half, step):
        pair, side = fine_at(half, step)
        fine_step(level0, level1, 0, pair + 2, side)

    def second_layer(half, step):
        pair, side = fine_at(half, step - 1)
        fine_step(level1, level2, 1, pair + 1, side)

    def third_layer(half, step):
        pair, side = fine_at(half, step - 2)
        fine_step(level2, fine, 2, pair, side)

    source_at = jnp.where(has_prev, 1, 0)
    def await_end(pair, side):
        end_copy(pair, side).wait_recv()

    def await_entering(half, step):
        pair, side = coarse_at(half, step)

        @pl.when((pair >= 4) & pick(side, has_above, has_below))
        def _():
            cold_halo(pair - 3, side).wait_recv()

        first = (half == 0) & (step == 0)

        @pl.when(has_prev & apart)
        def _():
            q = coarse_q(half, step)

            @pl.when(first)
            def _():
                await_end(*row_of(q + 1))
                await_end(*row_of(q))

            await_end(*row_of(jnp.where(half == 0, q - 1, q + 1)))

        @pl.when(has_prev & jnp.logical_not(apart))
        def _():
            @pl.when(first)
            def _():
                for early in (0, 1):
                    await_end(0, early)
                    await_end(1, early)

            @pl.when(step >= 2)
            def _():
                await_end(pair + 1, side)

    def coarse_row(half, step):
        pair, side = coarse_at(half, step)
        slot = slot_of(pair, side)
        value = conv_relu(field.at[source_at], weights[3], slot, 1)

        def row(ref):
            return ref[slot].astype(jnp.float32)

        leaving = value + (row(fine) - row(cold))
        store(end, slot, 1, jnp.where(in_image(pair, side), leaving, 0.0))
        store(coarse, slot, 1, value)

    def send_on(half, step):
        @pl.when(has_next)
        def _():
            end_copy(*coarse_at(half, step)).start()

    @pl.loop(0, halves)
    def _(half):
        def hand_back(ring):
            over_cut(ring).wait_recv()
            from_relay(ring).start()

        n_fine = jnp.where(apart, last, 2 * last)
        n_coarse = jnp.where(half == 0, 8 - 2 * layer, last + layer)
        n_coarse = jnp.where(apart, n_coarse, 2 * last + 2)
        lag = jnp.where(layer == 0, jnp.where(half == 0, 0, 2), LAG)
        lag = jnp.where(layer >= 2, n_fine + 2, lag)

        @pl.loop(0, jnp.minimum(lag, n_fine))
        def _(step):
            await_ring(half, step)
            third_layer(half, step)
            second_layer(half, step)
            first_layer(half, step)

        @pl.loop(lag, n_fine)
        def _(step):
            await_ring(half, step)
            await_entering(half, step - lag)
            third_layer(half, step)
            coarse_row(half, step - lag)
            second_layer(half, step)
            first_layer(half, step)
            send_on(half, step - lag)

        @pl.when(lag <= n_fine)
        def _():
            await_entering(half, n_fine - lag)
            third_layer(half, n_fine)
            coarse_row(half, n_fine - lag)
            second_layer(half, n_fine)
            send_on(half, n_fine - lag)
            await_entering(half, n_fine + 1 - lag)
            third_layer(half, n_fine + 1)
            coarse_row(half, n_fine + 1 - lag)
            send_on(half, n_fine + 1 - lag)

        @pl.when(lag > n_fine)
        def _():
            third_layer(half, n_fine)
            second_layer(half, n_fine)
            third_layer(half, n_fine + 1)

        rings(returns & (half == 0), 1, relayed + 1, hand_back)

        @pl.loop(n_fine + 2 - lag, n_coarse)
        def _(step):
            await_entering(half, step)
            coarse_row(half, step)
            send_on(half, step)

    rings(detours, 1, relayed + 1, lambda ring: to_relay(ring).wait_send())
    rings(relays, 1, relayed + 1, lambda ring: over_cut(ring).wait_send())
    rings(returns, 1, relayed + 1, lambda ring: from_relay(ring).wait_send())
    rings(
        to[0] & jnp.logical_not(detours), 1, last - 2,
        lambda ring: cold_halo(ring, 0).wait_send(),
    )
    rings(to[1], 1, last - 2, lambda ring: cold_halo(ring, 1).wait_send())
    for side in (0, 1):
        rings(to[side], 1, last + 1, lambda ring, side=side: field_halo(ring, side).wait_send())

        @pl.when(has_next)
        def _(side=side):
            @pl.loop(0, last + 1)
            def _(pair):
                end_copy(pair, side).wait_send()


def hand_over(end, coarse, end_out, coarse_out, sem):
    rows = pl.ds(RIM, end_out.shape[1])
    copies = [
        pltpu.make_async_copy(end.at[rows], end_out.at[0], sem.at[0]),
        pltpu.make_async_copy(coarse.at[rows], coarse_out.at[0], sem.at[1]),
    ]
    for copy in copies:
        copy.start()
    for copy in copies:
        copy.wait()


def per_device(states, coarse_old, fine_weights, coarse_weights):
    _, rows, cols, chans = states.shape
    out = jax.ShapeDtypeStruct(states.shape, states.dtype)
    image = (rows + 2 * RIM, cols, chans)
    bf16 = jnp.bfloat16
    dma = pltpu.SemaphoreType.DMA
    def stay(array):
        return pltpu.with_memory_space_constraint(array, pltpu.HBM)

    results = pl.pallas_call(
        kernel,
        out_shape=(jax.ShapeDtypeStruct(image, bf16),) * 2,
        in_specs=[pl.BlockSpec(memory_space=pl.ANY)] * 4,
        out_specs=[pl.BlockSpec(memory_space=pltpu.VMEM)] * 2,
        scratch_shapes=[
            pltpu.VMEM((2, *image), bf16),
            pltpu.VMEM(image, bf16),
            pltpu.VMEM(image, bf16),
            pltpu.VMEM(image, bf16),
            pltpu.VMEM(image, bf16),
            pltpu.VMEM((4, 3, 3, chans, chans), bf16),
            dma((2,)),
            dma((4, 3)),
            dma((2, 6)),
            dma((2, 6)),
            dma((2, 3)),
            dma((2, 3)),
            dma((2, 7)),
            dma((2, 7)),
            pltpu.VMEM((3, cols, chans), bf16),
            dma((3,)),
            dma((3,)),
            dma((3,)),
        ],
        compiler_params=pltpu.CompilerParams(
            vmem_limit_bytes=40 << 20, collective_id=0, has_side_effects=True
        ),
    )(
        stay(states),
        stay(coarse_old),
        stay(fine_weights.reshape(1, 3, 3, 3, chans, chans)),
        stay(coarse_weights.reshape(1, 3, 3, chans, chans)),
    )
    return pl.pallas_call(
        hand_over,
        out_shape=(out, out),
        in_specs=[pl.BlockSpec(memory_space=pl.ANY)] * 2,
        out_specs=[pl.BlockSpec(memory_space=pl.ANY)] * 2,
        scratch_shapes=[dma((2,))],
        compiler_params=pltpu.CompilerParams(vmem_limit_bytes=1 << 20),
    )(*results)


def solution(mesh):
    in_specs = (
        P("layer", "space", None, None),
        P("layer", "space", None, None),
        P("layer", None, None, None, None),
        P("layer", None, None, None),
    )
    out_specs = (P("layer", "space", None, None), P("layer", "space", None, None))
    return jax.shard_map(
        per_device, mesh=mesh, in_specs=in_specs, out_specs=out_specs, check_vma=False
    )
```

```python
import jax
import jax.numpy as jnp
from jax import lax
from jax.experimental import pallas as pl
from jax.experimental.pallas import tpu as pltpu
from jax.sharding import PartitionSpec as P

MESH = pl.DeviceIdType.MESH

RIM = 6
TOP, BOTTOM = RIM + 3, RIM + 4
LAG = 4


def conv_relu(source, weights, start, count):
    _, cols, chans = source.shape
    rows = count * cols
    taps = [
        source[pl.ds(start + row_step, count)].reshape(rows, chans)
        for row_step in (-1, 0, 1)
    ]
    window = jnp.concatenate(taps, axis=1)
    parts = [
        jnp.dot(
            window,
            weights[step].reshape(3 * chans, chans),
            preferred_element_type=jnp.float32,
        )
        for step in range(3)
    ]
    col = lax.broadcasted_iota(jnp.int32, (rows, chans), 0) % cols
    left = jnp.where(col == 0, 0.0, pltpu.roll(parts[0], 1, 0))
    right = jnp.where(col == cols - 1, 0.0, pltpu.roll(parts[2], rows - 1, 0))
    total = parts[1] + left + right
    return taps[1].astype(jnp.float32) + jnp.maximum(total, 0.0)


def kernel(
    states, coarse_old, fine_w, coarse_w, end, coarse,
    field, level1, level2, fine, cold, weights,
    load_sem, weight_sem, halo_send, halo_recv, cold_send, cold_recv,
    end_send, end_recv, relay, relay_send, relay_recv, forward_send,
):
    layer, space = lax.axis_index("layer"), lax.axis_index("space")
    groups, strips = lax.axis_size("layer"), lax.axis_size("space")
    cols = states.shape[2]
    has_above, has_below = space > 0, space < strips - 1
    has_prev, has_next = layer > 0, layer < groups - 1
    last = groups - 1 - layer + 3

    first_two = layer < 2
    partner = jnp.where(first_two, layer + 2, layer - 2)
    relayed = jnp.where(first_two, 3 - layer, 5 - layer)
    leaves, enters = space == strips // 2 - 1, space == strips // 2

    barrier = pltpu.get_barrier_semaphore()
    peers = (
        (has_above, (layer, space - 1)),
        (has_below, (layer, space + 1)),
        (has_prev, (layer - 1, space)),
        (has_next, (layer + 1, space)),
        (leaves | enters, (partner, space)),
    )
    for present, peer in peers:
        @pl.when(present)
        def _(peer=peer):
            pl.semaphore_signal(barrier, inc=1, device_id=peer, device_id_type=MESH)

    greeted = sum(present.astype(jnp.int32) for present, _ in peers)

    load_field = pltpu.make_async_copy(
        states.at[0], field.at[0, pl.ds(RIM, 8)], load_sem.at[0]
    )
    load_field.start()
    loads = []
    for which in range(4):
        source = coarse_w if which == 3 else fine_w.at[0, which]
        source = source.at[0] if which == 3 else source
        loads.append(
            [
                pltpu.make_async_copy(
                    source.at[:, step], weights.at[which, step], weight_sem.at[which, step]
                )
                for step in range(3)
            ]
        )
    for group in loads[:3]:
        for copy in group:
            copy.start()
    load_cold = pltpu.make_async_copy(
        coarse_old.at[0], cold.at[pl.ds(RIM, 8)], load_sem.at[1]
    )
    for copy in loads[3]:
        copy.start()
    load_cold.start()

    def pick(side, upper, lower):
        return jnp.where(side == 0, upper, lower)

    def slot_of(pair, side):
        return pick(side, TOP - pair, BOTTOM + pair)

    def halo(ring, side, array, target, send, recv):
        return pltpu.make_async_remote_copy(
            src_ref=array.at[0, pick(side, 8 - ring, ring - 1)],
            dst_ref=target.at[slot_of(3 + ring, side)],
            send_sem=send.at[side, ring - 1],
            recv_sem=recv.at[side, ring - 1],
            device_id=(layer, pick(side, space + 1, space - 1)),
            device_id_type=MESH,
        )

    def field_halo(ring, side):
        return halo(ring, side, states, field.at[0], halo_send, halo_recv)

    def cold_halo(ring, side):
        return halo(ring, side, coarse_old, cold, cold_send, cold_recv)

    def detour(ring, source, target, send, recv, device):
        return pltpu.make_async_remote_copy(
            src_ref=source,
            dst_ref=target,
            send_sem=send.at[ring - 1],
            recv_sem=recv,
            device_id=device,
            device_id_type=MESH,
        )

    def to_relay(ring):
        return detour(
            ring, coarse_old.at[0, 8 - ring], relay.at[ring - 1],
            relay_send, relay_recv.at[ring - 1], (partner, space),
        )

    def over_cut(ring):
        return detour(
            ring, relay.at[ring - 1], relay.at[ring - 1],
            forward_send, relay_recv.at[ring - 1], (layer, space + 1),
        )

    def from_relay(ring):
        return detour(
            ring, relay.at[ring - 1], cold.at[TOP - 3 - ring],
            forward_send, cold_recv.at[0, ring - 1], (partner, space),
        )

    def rings(condition, start, stop, act):
        @pl.when(condition)
        def _():
            @pl.loop(start, stop)
            def _(ring):
                act(ring)

    relays = leaves & jnp.logical_not(first_two)
    returns = enters & jnp.logical_not(first_two)
    detours = leaves & first_two

    def end_copy(pair, side):
        slot = slot_of(pair, side)
        return pltpu.make_async_remote_copy(
            src_ref=end.at[slot],
            dst_ref=field.at[1, slot],
            send_sem=end_send.at[side, pair],
            recv_sem=end_recv.at[side, pair],
            device_id=(layer + 1, space),
            device_id_type=MESH,
        )

    to = (has_below, has_above)

    def store(target, start, count, value):
        target[pl.ds(start, count)] = value.reshape(count, cols, -1).astype(target.dtype)

    def fine_rows(source, target, which, start, count):
        store(target, start, count, conv_relu(source, weights[which], start, count))

    def in_image(pair, side):
        return pick(side, has_above, has_below) | (pair <= 3)

    @pl.when(jnp.logical_not(has_above))
    def _():
        field[0, 0:RIM] = jnp.zeros((RIM, *field.shape[2:]), field.dtype)

    @pl.when(jnp.logical_not(has_below))
    def _():
        field[0, RIM + 8 :] = jnp.zeros((RIM, *field.shape[2:]), field.dtype)

    level0 = field.at[0]
    late = has_above & (space % 8 == 0)

    def prelude(part, carry):
        @pl.when((part == 0) != late)
        def _():
            pl.semaphore_wait(barrier, greeted)

            def pass_on(ring):
                to_relay(ring).wait_recv()
                over_cut(ring).start()

            split = jnp.where(relays, 3, last + 1)
            rings(detours, 2, relayed + 1, lambda ring: to_relay(ring).start())
            rings(to[0], 1, split, lambda ring: field_halo(ring, 0).start())
            rings(to[1], 1, last + 1, lambda ring: field_halo(ring, 1).start())
            rings(to[1], 1, last - 2, lambda ring: cold_halo(ring, 1).start())
            rings(relays, 2, relayed + 1, pass_on)
            rings(to[0], split, last + 1, lambda ring: field_halo(ring, 0).start())
            rings(
                to[0], jnp.where(detours, 1, 1), jnp.where(detours, 2, last - 2),
                lambda ring: cold_halo(ring, 0).start(),
            )

        @pl.when((part == 0) == late)
        def _():
            load_field.wait()
            for copy in loads[0]:
                copy.wait()
            for row in (1, 3, 5):
                fine_rows(level0, level1, 0, RIM + row, 2)
            for copy in loads[1]:
                copy.wait()
            for row in (2, 4):
                fine_rows(level1, level2, 1, RIM + row, 2)
            for copy in loads[2]:
                copy.wait()
            fine_rows(level2, fine, 2, RIM + 3, 2)
            for copy in loads[3]:
                copy.wait()
            load_cold.wait()

        return carry

    lax.fori_loop(0, 2, prelude, 0)

    apart = enters | (space == strips // 2 + 1)
    halves = jnp.where(apart, 2, 1)
    swap = (space % 8 <= 1).astype(jnp.int32)

    def row_of(q):
        return jnp.where(q >= 0, q, -1 - q), jnp.where(q >= 0, 0, 1)

    def fine_at(half, step):
        _, side = row_of(jnp.where(half == 0, -1, 0))
        pair = jnp.where(apart, step, step // 2) + 1
        return pair, jnp.where(apart, side, (step + swap) % 2)

    def coarse_q(half, step):
        return jnp.where(half == 0, -layer - step, step - layer + 1)

    def coarse_at(half, step):
        pair, side = row_of(coarse_q(half, step))
        return (
            jnp.where(apart, pair, step // 2),
            jnp.where(apart, side, (step + swap) % 2),
        )

    def fine_step(source, target, which, pair, side):
        slot = slot_of(pair, side)
        value = conv_relu(source, weights[which], slot, 1)
        store(target, slot, 1, jnp.where(in_image(pair, side), value, 0.0))

    def await_ring(half, step):
        ring, side = fine_at(half, step)

        @pl.when(pick(side, has_above, has_below))
        def _():
            field_halo(ring, side).wait_recv()

    def first_layer(half, step):
        pair, side = fine_at(half, step)
        fine_step(level0, level1, 0, pair + 2, side)

    def second_layer(half, step):
        pair, side = fine_at(half, step - 1)
        fine_step(level1, level2, 1, pair + 1, side)

    def third_layer(half, step):
        pair, side = fine_at(half, step - 2)
        fine_step(level2, fine, 2, pair, side)

    source_at = jnp.where(has_prev, 1, 0)
    def await_end(pair, side):
        end_copy(pair, side).wait_recv()

    def await_entering(half, step):
        pair, side = coarse_at(half, step)

        @pl.when((pair >= 4) & pick(side, has_above, has_below))
        def _():
            cold_halo(pair - 3, side).wait_recv()

        first = (half == 0) & (step == 0)

        @pl.when(has_prev & apart)
        def _():
            q = coarse_q(half, step)

            @pl.when(first)
            def _():
                await_end(*row_of(q + 1))
                await_end(*row_of(q))

            await_end(*row_of(jnp.where(half == 0, q - 1, q + 1)))

        @pl.when(has_prev & jnp.logical_not(apart))
        def _():
            @pl.when(first)
            def _():
                for early in (0, 1):
                    await_end(0, early)
                    await_end(1, early)

            @pl.when(step >= 2)
            def _():
                await_end(pair + 1, side)

    def coarse_row(half, step):
        pair, side = coarse_at(half, step)
        slot = slot_of(pair, side)
        value = conv_relu(field.at[source_at], weights[3], slot, 1)

        def row(ref):
            return ref[slot].astype(jnp.float32)

        leaving = value + (row(fine) - row(cold))
        store(end, slot, 1, jnp.where(in_image(pair, side), leaving, 0.0))
        store(coarse, slot, 1, value)

    def send_on(half, step):
        @pl.when(has_next)
        def _():
            end_copy(*coarse_at(half, step)).start()

    @pl.loop(0, halves)
    def _(half):
        def hand_back(ring):
            over_cut(ring).wait_recv()
            from_relay(ring).start()

        n_fine = jnp.where(apart, last, 2 * last)
        n_coarse = jnp.where(half == 0, 8 - 2 * layer, last + layer)
        n_coarse = jnp.where(apart, n_coarse, 2 * last + 2)
        lag = jnp.where(half == 0, jnp.where(layer == 0, 0, LAG), 2)
        lag = jnp.where(layer >= 2, n_fine + 2, lag)

        @pl.loop(0, jnp.minimum(lag, n_fine))
        def _(step):
            await_ring(half, step)
            third_layer(half, step)
            second_layer(half, step)
            first_layer(half, step)

        @pl.loop(lag, n_fine)
        def _(step):
            await_ring(half, step)
            await_entering(half, step - lag)
            third_layer(half, step)
            coarse_row(half, step - lag)
            second_layer(half, step)
            first_layer(half, step)
            send_on(half, step - lag)

        @pl.when(lag <= n_fine)
        def _():
            await_entering(half, n_fine - lag)
            third_layer(half, n_fine)
            coarse_row(half, n_fine - lag)
            second_layer(half, n_fine)
            send_on(half, n_fine - lag)
            await_entering(half, n_fine + 1 - lag)
            third_layer(half, n_fine + 1)
            coarse_row(half, n_fine + 1 - lag)
            send_on(half, n_fine + 1 - lag)

        @pl.when(lag > n_fine)
        def _():
            third_layer(half, n_fine)
            second_layer(half, n_fine)
            third_layer(half, n_fine + 1)

        rings(returns & (half == 0), 2, relayed + 1, hand_back)

        @pl.loop(n_fine + 2 - lag, n_coarse)
        def _(step):
            await_entering(half, step)
            coarse_row(half, step)
            send_on(half, step)

    rings(detours, 2, relayed + 1, lambda ring: to_relay(ring).wait_send())
    rings(relays, 2, relayed + 1, lambda ring: over_cut(ring).wait_send())
    rings(returns, 2, relayed + 1, lambda ring: from_relay(ring).wait_send())
    rings(
        to[0], jnp.where(detours, 1, 1), jnp.where(detours, 2, last - 2),
        lambda ring: cold_halo(ring, 0).wait_send(),
    )
    rings(to[1], 1, last - 2, lambda ring: cold_halo(ring, 1).wait_send())
    for side in (0, 1):
        rings(to[side], 1, last + 1, lambda ring, side=side: field_halo(ring, side).wait_send())

        @pl.when(has_next)
        def _(side=side):
            @pl.loop(0, last + 1)
            def _(pair):
                end_copy(pair, side).wait_send()


def hand_over(end, coarse, end_out, coarse_out, sem):
    rows = pl.ds(RIM, end_out.shape[1])
    copies = [
        pltpu.make_async_copy(end.at[rows], end_out.at[0], sem.at[0]),
        pltpu.make_async_copy(coarse.at[rows], coarse_out.at[0], sem.at[1]),
    ]
    for copy in copies:
        copy.start()
    for copy in copies:
        copy.wait()


def per_device(states, coarse_old, fine_weights, coarse_weights):
    _, rows, cols, chans = states.shape
    out = jax.ShapeDtypeStruct(states.shape, states.dtype)
    image = (rows + 2 * RIM, cols, chans)
    bf16 = jnp.bfloat16
    dma = pltpu.SemaphoreType.DMA
    def stay(array):
        return pltpu.with_memory_space_constraint(array, pltpu.HBM)

    results = pl.pallas_call(
        kernel,
        out_shape=(jax.ShapeDtypeStruct(image, bf16),) * 2,
        in_specs=[pl.BlockSpec(memory_space=pl.ANY)] * 4,
        out_specs=[pl.BlockSpec(memory_space=pltpu.VMEM)] * 2,
        scratch_shapes=[
            pltpu.VMEM((2, *image), bf16),
            pltpu.VMEM(image, bf16),
            pltpu.VMEM(image, bf16),
            pltpu.VMEM(image, bf16),
            pltpu.VMEM(image, bf16),
            pltpu.VMEM((4, 3, 3, chans, chans), bf16),
            dma((2,)),
            dma((4, 3)),
            dma((2, 6)),
            dma((2, 6)),
            dma((2, 3)),
            dma((2, 3)),
            dma((2, 7)),
            dma((2, 7)),
            pltpu.VMEM((3, cols, chans), bf16),
            dma((3,)),
            dma((3,)),
            dma((3,)),
        ],
        compiler_params=pltpu.CompilerParams(
            vmem_limit_bytes=40 << 20, collective_id=0, has_side_effects=True
        ),
    )(
        stay(states),
        stay(coarse_old),
        stay(fine_weights.reshape(1, 3, 3, 3, chans, chans)),
        stay(coarse_weights.reshape(1, 3, 3, chans, chans)),
    )
    return pl.pallas_call(
        hand_over,
        out_shape=(out, out),
        in_specs=[pl.BlockSpec(memory_space=pl.ANY)] * 2,
        out_specs=[pl.BlockSpec(memory_space=pl.ANY)] * 2,
        scratch_shapes=[dma((2,))],
        compiler_params=pltpu.CompilerParams(vmem_limit_bytes=1 << 20),
    )(*results)


def solution(mesh):
    in_specs = (
        P("layer", "space", None, None),
        P("layer", "space", None, None),
        P("layer", None, None, None, None),
        P("layer", None, None, None),
    )
    out_specs = (P("layer", "space", None, None), P("layer", "space", None, None))
    return jax.shard_map(
        per_device, mesh=mesh, in_specs=in_specs, out_specs=out_specs, check_vma=False
    )
```

```python
import jax
import jax.numpy as jnp
from jax import lax
from jax.experimental import pallas as pl
from jax.experimental.pallas import tpu as pltpu
from jax.sharding import PartitionSpec as P

MESH = pl.DeviceIdType.MESH

RIM = 6
TOP, BOTTOM = RIM + 3, RIM + 4
LAG = 4


def conv_relu(source, weights, start, count):
    _, cols, chans = source.shape
    rows = count * cols
    taps = [
        source[pl.ds(start + row_step, count)].reshape(rows, chans)
        for row_step in (-1, 0, 1)
    ]
    window = jnp.concatenate(taps, axis=1)
    parts = [
        jnp.dot(
            window,
            weights[step].reshape(3 * chans, chans),
            preferred_element_type=jnp.float32,
        )
        for step in range(3)
    ]
    col = lax.broadcasted_iota(jnp.int32, (rows, chans), 0) % cols
    left = jnp.where(col == 0, 0.0, pltpu.roll(parts[0], 1, 0))
    right = jnp.where(col == cols - 1, 0.0, pltpu.roll(parts[2], rows - 1, 0))
    total = parts[1] + left + right
    return taps[1].astype(jnp.float32) + jnp.maximum(total, 0.0)


def kernel(
    states, coarse_old, fine_w, coarse_w, end, coarse,
    field, level1, level2, fine, cold, weights,
    load_sem, weight_sem, halo_send, halo_recv, cold_send, cold_recv,
    end_send, end_recv, relay, relay_send, relay_recv, forward_send,
):
    layer, space = lax.axis_index("layer"), lax.axis_index("space")
    groups, strips = lax.axis_size("layer"), lax.axis_size("space")
    cols = states.shape[2]
    has_above, has_below = space > 0, space < strips - 1
    has_prev, has_next = layer > 0, layer < groups - 1
    last = groups - 1 - layer + 3

    first_two = layer < 2
    partner = jnp.where(first_two, layer + 2, layer - 2)
    relayed = jnp.where(first_two, 3 - layer, 5 - layer)
    leaves, enters = space == strips // 2 - 1, space == strips // 2

    barrier = pltpu.get_barrier_semaphore()
    peers = (
        (has_above, (layer, space - 1)),
        (has_below, (layer, space + 1)),
        (has_prev, (layer - 1, space)),
        (has_next, (layer + 1, space)),
        (leaves | enters, (partner, space)),
    )
    for present, peer in peers:
        @pl.when(present)
        def _(peer=peer):
            pl.semaphore_signal(barrier, inc=1, device_id=peer, device_id_type=MESH)

    greeted = sum(present.astype(jnp.int32) for present, _ in peers)

    load_field = pltpu.make_async_copy(
        states.at[0], field.at[0, pl.ds(RIM, 8)], load_sem.at[0]
    )
    load_field.start()
    loads = []
    for which in range(4):
        source = coarse_w if which == 3 else fine_w.at[0, which]
        source = source.at[0] if which == 3 else source
        loads.append(
            [
                pltpu.make_async_copy(
                    source.at[:, step], weights.at[which, step], weight_sem.at[which, step]
                )
                for step in range(3)
            ]
        )
    for group in loads[:3]:
        for copy in group:
            copy.start()
    load_cold = pltpu.make_async_copy(
        coarse_old.at[0], cold.at[pl.ds(RIM, 8)], load_sem.at[1]
    )
    for copy in loads[3]:
        copy.start()
    load_cold.start()

    def pick(side, upper, lower):
        return jnp.where(side == 0, upper, lower)

    def slot_of(pair, side):
        return pick(side, TOP - pair, BOTTOM + pair)

    def halo(ring, side, array, target, send, recv):
        return pltpu.make_async_remote_copy(
            src_ref=array.at[0, pick(side, 8 - ring, ring - 1)],
            dst_ref=target.at[slot_of(3 + ring, side)],
            send_sem=send.at[side, ring - 1],
            recv_sem=recv.at[side, ring - 1],
            device_id=(layer, pick(side, space + 1, space - 1)),
            device_id_type=MESH,
        )

    def field_halo(ring, side):
        return halo(ring, side, states, field.at[0], halo_send, halo_recv)

    def cold_halo(ring, side):
        return halo(ring, side, coarse_old, cold, cold_send, cold_recv)

    def detour(ring, source, target, send, recv, device):
        return pltpu.make_async_remote_copy(
            src_ref=source,
            dst_ref=target,
            send_sem=send.at[ring - 1],
            recv_sem=recv,
            device_id=device,
            device_id_type=MESH,
        )

    def to_relay(ring):
        return detour(
            ring, coarse_old.at[0, 8 - ring], relay.at[ring - 1],
            relay_send, relay_recv.at[ring - 1], (partner, space),
        )

    def over_cut(ring):
        return detour(
            ring, relay.at[ring - 1], relay.at[ring - 1],
            forward_send, relay_recv.at[ring - 1], (layer, space + 1),
        )

    def from_relay(ring):
        return detour(
            ring, relay.at[ring - 1], cold.at[TOP - 3 - ring],
            forward_send, cold_recv.at[0, ring - 1], (partner, space),
        )

    def rings(condition, start, stop, act):
        @pl.when(condition)
        def _():
            @pl.loop(start, stop)
            def _(ring):
                act(ring)

    def send_cold(condition):
        stop = jnp.where(detours, 2, last - 2)
        rings(to[0] & condition, 1, stop, lambda ring: cold_halo(ring, 0).start())
        rings(to[1] & condition, 1, last - 2, lambda ring: cold_halo(ring, 1).start())

    relays = leaves & jnp.logical_not(first_two)
    returns = enters & jnp.logical_not(first_two)
    detours = leaves & first_two

    def end_copy(pair, side):
        slot = slot_of(pair, side)
        return pltpu.make_async_remote_copy(
            src_ref=end.at[slot],
            dst_ref=field.at[1, slot],
            send_sem=end_send.at[side, pair],
            recv_sem=end_recv.at[side, pair],
            device_id=(layer + 1, space),
            device_id_type=MESH,
        )

    to = (has_below, has_above)

    def store(target, start, count, value):
        target[pl.ds(start, count)] = value.reshape(count, cols, -1).astype(target.dtype)

    def fine_rows(source, target, which, start, count):
        store(target, start, count, conv_relu(source, weights[which], start, count))

    def in_image(pair, side):
        return pick(side, has_above, has_below) | (pair <= 3)

    @pl.when(jnp.logical_not(has_above))
    def _():
        field[0, 0:RIM] = jnp.zeros((RIM, *field.shape[2:]), field.dtype)

    @pl.when(jnp.logical_not(has_below))
    def _():
        field[0, RIM + 8 :] = jnp.zeros((RIM, *field.shape[2:]), field.dtype)

    level0 = field.at[0]
    late = has_above & (space % 8 == 0)

    def prelude(part, carry):
        @pl.when((part == 0) != late)
        def _():
            pl.semaphore_wait(barrier, greeted)

            def pass_on(ring):
                to_relay(ring).wait_recv()
                over_cut(ring).start()

            split = jnp.where(relays, 3, last + 1)
            rings(detours, 2, relayed + 1, lambda ring: to_relay(ring).start())
            rings(to[0], 1, split, lambda ring: field_halo(ring, 0).start())
            rings(to[1], 1, last + 1, lambda ring: field_halo(ring, 1).start())
            rings(relays, 2, relayed + 1, pass_on)
            rings(to[0], split, last + 1, lambda ring: field_halo(ring, 0).start())
            send_cold(layer != 1)

        @pl.when((part == 0) == late)
        def _():
            load_field.wait()
            for copy in loads[0]:
                copy.wait()
            for row in (1, 3, 5):
                fine_rows(level0, level1, 0, RIM + row, 2)
            for copy in loads[1]:
                copy.wait()
            for row in (2, 4):
                fine_rows(level1, level2, 1, RIM + row, 2)
            for copy in loads[2]:
                copy.wait()
            fine_rows(level2, fine, 2, RIM + 3, 2)
            for copy in loads[3]:
                copy.wait()
            load_cold.wait()

        return carry

    lax.fori_loop(0, 2, prelude, 0)

    apart = enters | (space == strips // 2 + 1)
    halves = jnp.where(apart, 2, 1)
    swap = (space % 8 <= 1).astype(jnp.int32)

    def row_of(q):
        return jnp.where(q >= 0, q, -1 - q), jnp.where(q >= 0, 0, 1)

    def fine_at(half, step):
        _, side = row_of(jnp.where(half == 0, -1, 0))
        pair = jnp.where(apart, step, step // 2) + 1
        return pair, jnp.where(apart, side, (step + swap) % 2)

    def coarse_q(half, step):
        return jnp.where(half == 0, -layer - step, step - layer + 1)

    def coarse_at(half, step):
        pair, side = row_of(coarse_q(half, step))
        return (
            jnp.where(apart, pair, step // 2),
            jnp.where(apart, side, (step + swap) % 2),
        )

    def fine_step(source, target, which, pair, side):
        slot = slot_of(pair, side)
        value = conv_relu(source, weights[which], slot, 1)
        store(target, slot, 1, jnp.where(in_image(pair, side), value, 0.0))

    def await_ring(half, step):
        ring, side = fine_at(half, step)

        @pl.when(pick(side, has_above, has_below))
        def _():
            field_halo(ring, side).wait_recv()

    def first_layer(half, step):
        pair, side = fine_at(half, step)
        fine_step(level0, level1, 0, pair + 2, side)

    def second_layer(half, step):
        pair, side = fine_at(half, step - 1)
        fine_step(level1, level2, 1, pair + 1, side)

    def third_layer(half, step):
        pair, side = fine_at(half, step - 2)
        fine_step(level2, fine, 2, pair, side)

    source_at = jnp.where(has_prev, 1, 0)
    def await_end(pair, side):
        end_copy(pair, side).wait_recv()

    def await_entering(half, step):
        pair, side = coarse_at(half, step)

        @pl.when((pair >= 4) & pick(side, has_above, has_below))
        def _():
            cold_halo(pair - 3, side).wait_recv()

        first = (half == 0) & (step == 0)

        @pl.when(has_prev & apart)
        def _():
            q = coarse_q(half, step)

            @pl.when(first)
            def _():
                await_end(*row_of(q + 1))
                await_end(*row_of(q))

            await_end(*row_of(jnp.where(half == 0, q - 1, q + 1)))

        @pl.when(has_prev & jnp.logical_not(apart))
        def _():
            @pl.when(first)
            def _():
                for early in (0, 1):
                    await_end(0, early)
                    await_end(1, early)

            @pl.when(step >= 2)
            def _():
                await_end(pair + 1, side)

    def coarse_row(half, step):
        pair, side = coarse_at(half, step)
        slot = slot_of(pair, side)
        value = conv_relu(field.at[source_at], weights[3], slot, 1)

        def row(ref):
            return ref[slot].astype(jnp.float32)

        leaving = value + (row(fine) - row(cold))
        store(end, slot, 1, jnp.where(in_image(pair, side), leaving, 0.0))
        store(coarse, slot, 1, value)

    def send_on(half, step):
        @pl.when(has_next)
        def _():
            end_copy(*coarse_at(half, step)).start()

    @pl.loop(0, halves)
    def _(half):
        def hand_back(ring):
            over_cut(ring).wait_recv()
            from_relay(ring).start()

        n_fine = jnp.where(apart, last, 2 * last)
        n_coarse = jnp.where(half == 0, 8 - 2 * layer, last + layer)
        n_coarse = jnp.where(apart, n_coarse, 2 * last + 2)
        lag = jnp.where(half == 0, jnp.where(layer == 0, 0, LAG), 2)
        lag = jnp.where(layer >= 2, n_fine + 2, lag)

        @pl.loop(0, jnp.minimum(lag, n_fine))
        def _(step):
            await_ring(half, step)
            third_layer(half, step)
            second_layer(half, step)
            first_layer(half, step)

        send_cold((layer == 1) & (half == 0))

        @pl.loop(lag, n_fine)
        def _(step):
            await_ring(half, step)
            await_entering(half, step - lag)
            third_layer(half, step)
            coarse_row(half, step - lag)
            second_layer(half, step)
            first_layer(half, step)
            send_on(half, step - lag)

        @pl.when(lag <= n_fine)
        def _():
            await_entering(half, n_fine - lag)
            third_layer(half, n_fine)
            coarse_row(half, n_fine - lag)
            second_layer(half, n_fine)
            send_on(half, n_fine - lag)
            await_entering(half, n_fine + 1 - lag)
            third_layer(half, n_fine + 1)
            coarse_row(half, n_fine + 1 - lag)
            send_on(half, n_fine + 1 - lag)

        @pl.when(lag > n_fine)
        def _():
            third_layer(half, n_fine)
            second_layer(half, n_fine)
            third_layer(half, n_fine + 1)

        rings(returns & (half == 0), 2, relayed + 1, hand_back)

        @pl.loop(n_fine + 2 - lag, n_coarse)
        def _(step):
            await_entering(half, step)
            coarse_row(half, step)
            send_on(half, step)

    rings(detours, 2, relayed + 1, lambda ring: to_relay(ring).wait_send())
    rings(relays, 2, relayed + 1, lambda ring: over_cut(ring).wait_send())
    rings(returns, 2, relayed + 1, lambda ring: from_relay(ring).wait_send())
    rings(
        to[0], jnp.where(detours, 1, 1), jnp.where(detours, 2, last - 2),
        lambda ring: cold_halo(ring, 0).wait_send(),
    )
    rings(to[1], 1, last - 2, lambda ring: cold_halo(ring, 1).wait_send())
    for side in (0, 1):
        rings(to[side], 1, last + 1, lambda ring, side=side: field_halo(ring, side).wait_send())

        @pl.when(has_next)
        def _(side=side):
            @pl.loop(0, last + 1)
            def _(pair):
                end_copy(pair, side).wait_send()


def hand_over(end, coarse, end_out, coarse_out, sem):
    rows = pl.ds(RIM, end_out.shape[1])
    copies = [
        pltpu.make_async_copy(end.at[rows], end_out.at[0], sem.at[0]),
        pltpu.make_async_copy(coarse.at[rows], coarse_out.at[0], sem.at[1]),
    ]
    for copy in copies:
        copy.start()
    for copy in copies:
        copy.wait()


def per_device(states, coarse_old, fine_weights, coarse_weights):
    _, rows, cols, chans = states.shape
    out = jax.ShapeDtypeStruct(states.shape, states.dtype)
    image = (rows + 2 * RIM, cols, chans)
    bf16 = jnp.bfloat16
    dma = pltpu.SemaphoreType.DMA
    def stay(array):
        return pltpu.with_memory_space_constraint(array, pltpu.HBM)

    results = pl.pallas_call(
        kernel,
        out_shape=(jax.ShapeDtypeStruct(image, bf16),) * 2,
        in_specs=[pl.BlockSpec(memory_space=pl.ANY)] * 4,
        out_specs=[pl.BlockSpec(memory_space=pltpu.VMEM)] * 2,
        scratch_shapes=[
            pltpu.VMEM((2, *image), bf16),
            pltpu.VMEM(image, bf16),
            pltpu.VMEM(image, bf16),
            pltpu.VMEM(image, bf16),
            pltpu.VMEM(image, bf16),
            pltpu.VMEM((4, 3, 3, chans, chans), bf16),
            dma((2,)),
            dma((4, 3)),
            dma((2, 6)),
            dma((2, 6)),
            dma((2, 3)),
            dma((2, 3)),
            dma((2, 7)),
            dma((2, 7)),
            pltpu.VMEM((3, cols, chans), bf16),
            dma((3,)),
            dma((3,)),
            dma((3,)),
        ],
        compiler_params=pltpu.CompilerParams(
            vmem_limit_bytes=40 << 20, collective_id=0, has_side_effects=True
        ),
    )(
        stay(states),
        stay(coarse_old),
        stay(fine_weights.reshape(1, 3, 3, 3, chans, chans)),
        stay(coarse_weights.reshape(1, 3, 3, chans, chans)),
    )
    return pl.pallas_call(
        hand_over,
        out_shape=(out, out),
        in_specs=[pl.BlockSpec(memory_space=pl.ANY)] * 2,
        out_specs=[pl.BlockSpec(memory_space=pl.ANY)] * 2,
        scratch_shapes=[dma((2,))],
        compiler_params=pltpu.CompilerParams(vmem_limit_bytes=1 << 20),
    )(*results)


def solution(mesh):
    in_specs = (
        P("layer", "space", None, None),
        P("layer", "space", None, None),
        P("layer", None, None, None, None),
        P("layer", None, None, None),
    )
    out_specs = (P("layer", "space", None, None), P("layer", "space", None, None))
    return jax.shard_map(
        per_device, mesh=mesh, in_specs=in_specs, out_specs=out_specs, check_vma=False
    )
```
